1024 devices in a mesh: blk: 16 (over y_hi, x, core), uly: 4 (over y_lo), batch: 16 (over z).
Axes of the slice: x: 4, y: 8 (y_hi: 2, y_lo: 4; y = y_hi * 4 + y_lo), z: 16, core: 2. Of those that a mesh axis runs over, the one named last changes fastest.
Arguments:
- queries: bfloat16 [131072, 1024], P(('batch', 'blk', 'uly')), parts along dimension 0, may hold values from -10 to 10
- keys: bfloat16 [131072, 1024], P(('batch', 'blk', 'uly')), parts along dimension 0, may hold values from -10 to 10
- values: bfloat16 [131072, 1024], P(('batch', 'blk', 'uly')), parts along dimension 0, may hold values from -6 to 6
- out_grad: bfloat16 [131072, 1024], P(('batch', 'blk', 'uly')), parts along dimension 0, may hold values from -16 to 16
- block_mask: int32 [1024, 64], P('batch'), parts along dimension 0, may hold values from 0 to 1, as said below
Outputs:
- query_grad: bfloat16 [131072, 1024], P(('batch', 'blk', 'uly')), parts along dimension 0
- key_grad: bfloat16 [131072, 1024], P(('batch', 'blk', 'uly')), parts along dimension 0
- value_grad: bfloat16 [131072, 1024], P(('batch', 'blk', 'uly')), parts along dimension 0
The draws below stay inside these ranges and needn't reach their ends.
There are 16 independent parts, one for each index of `batch`. The reference program is written for one: setup_inputs(seed, part) draws one part's arguments, and reference() takes and returns one part's arrays. A program takes and returns all parts, laid end to end along the dimension named above; each array names one. Nothing has to cross between parts.
Inputs may be any that keep to these rules, and one draw needn't show every extreme that they name: block_mask[a, b] is 1 for every two blocks a, b of the same cell (cell c holds tokens c * 512 to (c + 1) * 512 - 1); for blocks of different cells it is 1 only where the two cells are neighbours on the closed chain of 16 cells (cell c beside cells c - 1 and c + 1 modulo 16), and 0 for all other pairs.
All inputs are finite; a program needn't handle non-finite values.
Results may differ from the reference program's by a relative error of at most 0.0096.
Values may be sent and summed in bfloat16 or wider, within the bound.
A program may use at most 32 MiB of HBM per device.

```python
import math
import jax
import jax.numpy as jnp
from jax import lax

HEADS = 8
HEAD_DIM = 128
HD = 1024
GENES = 512
CELLS = 16
TOKENS = 8192


def draw_queries(key, part):
    base_key = jax.random.fold_in(key, 1)
    base = jnp.clip(1.5 * jax.random.normal(base_key, (TOKENS, HEADS * HEAD_DIM), jnp.float32), -9.0, 9.0)
    return base.astype(jnp.bfloat16)


def draw_keys(key, part):
    base_key = jax.random.fold_in(key, 2)
    base = jnp.clip(jax.random.normal(base_key, (TOKENS, HEADS * HEAD_DIM), jnp.float32), -6.0, 6.0)
    return base.astype(jnp.bfloat16)


def draw_block_mask(key, part):
    count = TOKENS // 128
    per_cell = GENES // 128
    blocks = jnp.arange(count, dtype=jnp.int32)
    owner = blocks // per_cell
    inside = blocks % per_cell
    levels = jax.random.randint(jax.random.fold_in(key, 11), (CELLS, 2), 1, 9)
    coins = jax.random.randint(jax.random.fold_in(key, 12), (count, count), 0, 16)
    query_cell = owner[:, None]
    key_cell = owner[None, :]
    right = key_cell == (query_cell + 1) % CELLS
    left = key_cell == (query_cell - 1 + CELLS) % CELLS
    level = jnp.where(right, levels[owner, 0][:, None], levels[owner, 1][:, None])
    cross = (right | left) & (coins < level)
    forced = right & (inside[:, None] == per_cell - 1) & (inside[None, :] == 0)
    if per_cell > 1:
        forced = forced | left & (inside[:, None] == 0) & (inside[None, :] == per_cell - 1)
    same = query_cell == key_cell
    return (same | cross | forced).astype(jnp.int32)


def level_of(rng, shape, split, least, top_value):
    factor_of = 1.0
    for dim, blocks in split:
        heights = jax.random.uniform(jax.random.fold_in(jax.random.fold_in(rng, 6), dim), (blocks,), jnp.float32, least / len(split), top_value / len(split))
        factor_of = factor_of * jnp.repeat(jnp.exp(heights), shape[dim] // blocks).reshape((-1,) + (1,) * (len(shape) - 1 - dim))
    return factor_of


def scatter_about(own_key, dims, width, reach, split=(), kind=jnp.bfloat16):
    factor_of = level_of(own_key, dims, split, -0.22, 0.18) if split else 1.0
    values = jax.random.normal(own_key, dims, jnp.float32) * width * factor_of
    return jnp.minimum(jnp.maximum(values, -reach), reach).astype(kind)


def setup_inputs(seed: int = 0, part: int = 0) -> dict:
    key_of = jax.random.split(jax.random.key(seed), 6)
    part_keys = jax.random.split(jax.random.fold_in(key_of[5], part), 6)
    return {
        "queries": draw_queries(jax.random.fold_in(jax.random.fold_in(key_of[5], part), 71), part),
        "keys": draw_keys(jax.random.fold_in(jax.random.fold_in(key_of[5], part), 71), part),
        "values": scatter_about(part_keys[2], (TOKENS, HD), 1.0, 6.0, ((0, 64),)),
        "out_grad": scatter_about(part_keys[3], (TOKENS, HD), 4.0, 16.0, ((0, 64),)),
        "block_mask": draw_block_mask(jax.random.fold_in(jax.random.fold_in(key_of[5], part), 71), part),
    }


def band_cells(x, axis):
    return jnp.concatenate([jnp.roll(x, 1, axis=0), x, jnp.roll(x, -1, axis=0)], axis=axis)

def widen(mask_blocks):
    return jnp.repeat(jnp.repeat(mask_blocks, 128, axis=1), 128, axis=2)

def reference(queries, keys, values, out_grad, block_mask):
    per_cell = GENES // 128
    scale = 1.0 / math.sqrt(HEAD_DIM)

    def cells(x):
        return x.reshape(CELLS, GENES, HEADS, HEAD_DIM)
    q_cells = cells(queries)
    k_cells = cells(keys)
    v_cells = cells(values)
    g_cells = cells(out_grad)
    grid = (block_mask > 0).reshape(CELLS, per_cell, CELLS, per_cell)
    base = jnp.arange(CELLS, dtype=jnp.int32)
    near = (base[:, None] + jnp.array([-1, 0, 1], dtype=jnp.int32)[None, :]) % CELLS
    row_blocks = grid[base[:, None], :, near, :]
    row_blocks = jnp.transpose(row_blocks, (0, 2, 1, 3)).reshape(CELLS, per_cell, 3 * per_cell)
    row_mask = widen(row_blocks)
    col_blocks = grid[near, :, base[:, None], :].reshape(CELLS, 3 * per_cell, per_cell)
    col_mask = widen(col_blocks)

    def query_side(items):
        q_cell, k_band, v_band, g_cell, mask = items
        scores = jnp.einsum('qhd,khd->hqk', q_cell.astype(jnp.float32), k_band.astype(jnp.float32)) * scale
        scores = jnp.where(mask[None], scores, -1e+30)
        top = lax.optimization_barrier(jnp.max(scores, axis=-1, keepdims=True))
        total = lax.optimization_barrier(jnp.sum(jnp.where(mask[None], jnp.exp(scores - top), 0.0), axis=-1, keepdims=True))
        lse = top + jnp.log(total)
        probs = jnp.where(mask[None], jnp.exp(scores - lse), 0.0)
        dprobs = jnp.einsum('qhd,khd->hqk', g_cell.astype(jnp.float32), v_band.astype(jnp.float32))
        delta = lax.optimization_barrier(jnp.sum(probs * dprobs, axis=-1, keepdims=True))
        dscores = lax.optimization_barrier((probs * (dprobs - delta)).astype(jnp.bfloat16))
        grad = jnp.einsum('hqk,khd->qhd', dscores.astype(jnp.float32), k_band.astype(jnp.float32)) * scale
        return (grad.astype(jnp.bfloat16), lse[..., 0], delta[..., 0])
    q_grad, lse_all, delta_all = lax.map(query_side, (q_cells, band_cells(k_cells, 1), band_cells(v_cells, 1), g_cells, row_mask))

    def key_side(items):
        q_band, g_band, lse_band, delta_band, k_cell, v_cell, mask = items
        scores = jnp.einsum('qhd,khd->hqk', q_band.astype(jnp.float32), k_cell.astype(jnp.float32)) * scale
        probs = jnp.where(mask[None], jnp.exp(scores - lse_band[..., None]), 0.0)
        dprobs = jnp.einsum('qhd,khd->hqk', g_band.astype(jnp.float32), v_cell.astype(jnp.float32))
        dscores = lax.optimization_barrier((probs * (dprobs - delta_band[..., None])).astype(jnp.bfloat16))
        probs_low = lax.optimization_barrier(probs.astype(jnp.bfloat16))
        k_grad = jnp.einsum('hqk,qhd->khd', dscores.astype(jnp.float32), q_band.astype(jnp.float32)) * scale
        v_grad = jnp.einsum('hqk,qhd->khd', probs_low.astype(jnp.float32), g_band.astype(jnp.float32))
        return (k_grad.astype(jnp.bfloat16), v_grad.astype(jnp.bfloat16))
    k_grad, v_grad = lax.map(key_side, (band_cells(q_cells, 1), band_cells(g_cells, 1), band_cells(lse_all, 2), band_cells(delta_all, 2), k_cells, v_cells, col_mask))
    shape = (TOKENS, HEADS * HEAD_DIM)
    return (q_grad.reshape(shape), k_grad.reshape(shape), v_grad.reshape(shape))
```

```python
import functools
import math

import jax
import jax.numpy as jnp
from jax import lax
from jax.experimental import pallas as pl
from jax.experimental.pallas import tpu as pltpu
from jax.sharding import PartitionSpec as P

MESH = pl.DeviceIdType.MESH
DIM = 128
BLOCK = 128
HEADS_HERE = 2
F32 = jnp.float32
BF16 = jnp.bfloat16


def times_t(left, right):
    return lax.dot_general(left, right, (((1,), (1,)), ((), ())), preferred_element_type=F32)


def groups_sum(block):
    rows, columns = block.shape
    return jnp.sum(block.reshape(rows // 8, 8, columns), axis=0)


def groups_max(block):
    rows, columns = block.shape
    return jnp.max(block.reshape(rows // 8, 8, columns), axis=0)


def kernel(
    cells,
    ulys,
    q_hbm,
    k_hbm,
    v_hbm,
    g_hbm,
    mask_hbm,
    dq_hbm,
    dk_hbm,
    dv_hbm,
    kv,
    qg,
    scores,
    dprobs,
    probs_low,
    dscores,
    own,
    sides,
    landed,
    results,
    mask,
    mask_sem,
    local_sem,
    in_send,
    in_recv,
    band_send,
    band_recv,
    part_send,
    part_recv,
    out_local,
    out_send,
    out_recv,
):
    b = lax.axis_index("blk")
    u = lax.axis_index("uly")
    rows = q_hbm.shape[0]
    genes = rows * ulys
    per_cell = genes // BLOCK
    half = cells // 2

    def group_of(blk, uly):
        upper = blk // half
        return uly + upper * (ulys - 1 - 2 * uly)

    prior = lax.rem(b + cells - 1, cells)
    following = lax.rem(b + 1, cells)
    my_group = group_of(b, u)
    prior_uly = group_of(prior, my_group)
    following_uly = group_of(following, my_group)
    sideways = (
        {"blk": prior, "uly": prior_uly},
        {"blk": following, "uly": following_uly},
    )

    def peer(step):
        return lax.rem(u + step, ulys)

    barrier = pltpu.get_barrier_semaphore()
    for step in range(1, ulys):
        pl.semaphore_signal(
            barrier, inc=1, device_id={"uly": peer(step)}, device_id_type=MESH
        )
    for side in sideways:
        pl.semaphore_signal(barrier, inc=1, device_id=side, device_id_type=MESH)

    mask_rows = (b * per_cell // 8) * 8
    mask_copy = pltpu.make_async_copy(
        mask_hbm.at[pl.ds(pl.multiple_of(mask_rows, 8), 8), :], mask, mask_sem
    )
    mask_copy.start()

    sources = (k_hbm, v_hbm, q_hbm, g_hbm)

    def landing(head, which, uly):
        at = pl.ds(pl.multiple_of(uly * rows, rows), rows)
        if which < 2:
            return kv.at[head, which, 1, at, :]
        return qg.at[head, which - 2, at, :]

    def columns_of(group, head):
        start = (group * HEADS_HERE + head) * DIM
        return pl.ds(pl.multiple_of(start, DIM), DIM)

    def entry_local(head, which):
        return pltpu.make_async_copy(
            sources[which].at[:, columns_of(my_group, head)],
            landing(head, which, u),
            local_sem.at[head, which],
        )

    def entry_copy(head, which, step):
        to = peer(step)
        return pltpu.make_async_remote_copy(
            src_ref=sources[which].at[:, columns_of(group_of(b, to), head)],
            dst_ref=landing(head, which, u),
            send_sem=in_send.at[head, which, step - 1],
            recv_sem=in_recv.at[head, which, step - 1],
            device_id={"uly": to},
            device_id_type=MESH,
        )

    def entry_arrival(head, which, step):
        came_from = lax.rem(u + ulys - step, ulys)
        return pltpu.make_async_remote_copy(
            src_ref=sources[which].at[:, columns_of(my_group, head)],
            dst_ref=landing(head, which, came_from),
            send_sem=in_send.at[head, which, step - 1],
            recv_sem=in_recv.at[head, which, step - 1],
            device_id={"uly": came_from},
            device_id_type=MESH,
        )

    for head in range(HEADS_HERE):
        for which in range(4):
            entry_local(head, which).start()

    pl.semaphore_wait(barrier, ulys + 1)

    for head in range(HEADS_HERE):
        for which in range(4):
            for step in range(1, ulys):
                entry_copy(head, which, step).start()

    def await_entry(head, which):
        entry_local(head, which).wait()
        for step in range(1, ulys):
            entry_arrival(head, which, step).wait_recv()

    def band_copy(head, which, side):
        return pltpu.make_async_remote_copy(
            src_ref=kv.at[head, which, 1],
            dst_ref=kv.at[head, which, 2 - 2 * side],
            send_sem=band_send.at[head, which, side],
            recv_sem=band_recv.at[head, which, side],
            device_id=sideways[side],
            device_id_type=MESH,
        )

    def band_arrival(head, which, side):
        return pltpu.make_async_remote_copy(
            src_ref=kv.at[head, which, 1],
            dst_ref=kv.at[head, which, 2 - 2 * side],
            send_sem=band_send.at[head, which, side],
            recv_sem=band_recv.at[head, which, side],
            device_id=sideways[side],
            device_id_type=MESH,
        )

    def send_band(head):
        for which in range(2):
            await_entry(head, which)
            for side in range(2):
                band_copy(head, which, side).start()

    def part_copy(head, which, side):
        return pltpu.make_async_remote_copy(
            src_ref=sides.at[head, which, side],
            dst_ref=landed.at[head, which, 1 - side],
            send_sem=part_send.at[head, which, side],
            recv_sem=part_recv.at[head, which, side],
            device_id=sideways[side],
            device_id_type=MESH,
        )

    outs = (dq_hbm, dk_hbm, dv_hbm)

    def exit_local(head, which):
        return pltpu.make_async_copy(
            results.at[head, which, pl.ds(pl.multiple_of(u * rows, rows), rows), :],
            outs[which].at[:, columns_of(my_group, head)],
            out_local.at[head, which],
        )

    def exit_copy(head, which, step):
        to = peer(step)
        return pltpu.make_async_remote_copy(
            src_ref=results.at[head, which, pl.ds(pl.multiple_of(to * rows, rows), rows), :],
            dst_ref=outs[which].at[:, columns_of(my_group, head)],
            send_sem=out_send.at[head, which, step - 1],
            recv_sem=out_recv.at[head, which, step - 1],
            device_id={"uly": to},
            device_id_type=MESH,
        )

    def exit_arrival(head, which, step):
        came_from = lax.rem(u + ulys - step, ulys)
        return pltpu.make_async_remote_copy(
            src_ref=results.at[head, which, pl.ds(0, rows), :],
            dst_ref=outs[which].at[:, columns_of(group_of(b, came_from), head)],
            send_sem=out_send.at[head, which, step - 1],
            recv_sem=out_recv.at[head, which, step - 1],
            device_id={"uly": came_from},
            device_id_type=MESH,
        )

    def send_out(head, which):
        exit_local(head, which).start()
        for step in range(1, ulys):
            exit_copy(head, which, step).start()

    scale = 1.0 / math.sqrt(DIM)
    scale2 = scale * math.log2(math.e)
    first_row = lax.rem(b * per_cell, 8)
    near = (prior, b, following)

    def bias_row(part, block):
        pieces = []
        for a in range(per_cell):
            allowed = mask[first_row + a, near[part] * per_cell + block] > 0
            pieces.append(jnp.full((1, BLOCK), jnp.where(allowed, 0.0, -1e30), F32))
        return jnp.concatenate(pieces, axis=1)

    parts = [(part, block) for part in range(3) for block in range(per_cell)]

    def compute(head):
        q = qg[head, 0]
        g = qg[head, 1]
        top = None
        for part, block in parts:
            at = slice(block * BLOCK, (block + 1) * BLOCK)
            s = times_t(kv[head, 0, part, at, :], q) * scale2 + bias_row(part, block)
            scores[part, at, :] = s
            here = groups_max(s)
            top = here if top is None else jnp.maximum(top, here)
            dprobs[part, at, :] = times_t(kv[head, 1, part, at, :], g)
        top = jnp.max(top, axis=0, keepdims=True)
        total = jnp.zeros((8, genes), F32)
        delta = jnp.zeros((8, genes), F32)
        for part, block in parts:
            at = slice(block * BLOCK, (block + 1) * BLOCK)
            e = jnp.exp2(scores[part, at, :] - top)
            scores[part, at, :] = e
            total += groups_sum(e)
            delta += groups_sum(e * dprobs[part, at, :])
        inverse = 1.0 / jnp.sum(total, axis=0, keepdims=True)
        delta = jnp.sum(delta, axis=0, keepdims=True) * inverse
        for part, block in parts:
            at = slice(block * BLOCK, (block + 1) * BLOCK)
            p = scores[part, at, :] * inverse
            probs_low[part, at, :] = p.astype(BF16)
            dscores[part, at, :] = (p * (dprobs[part, at, :] - delta)).astype(BF16)
        for side in range(2):
            sides[head, 0, side] = jnp.dot(
                dscores[2 * side], q, preferred_element_type=F32
            ).astype(BF16)
            part_copy(head, 0, side).start()
            sides[head, 1, side] = jnp.dot(
                probs_low[2 * side], g, preferred_element_type=F32
            ).astype(BF16)
            part_copy(head, 1, side).start()
        grad = jnp.zeros((DIM, genes), F32)
        for part in range(3):
            grad += jnp.dot(kv[head, 0, part].T, dscores[part], preferred_element_type=F32)
        results[head, 0] = (grad.T * scale).astype(BF16)
        send_out(head, 0)
        own[head, 0] = jnp.dot(dscores[1], q, preferred_element_type=F32)
        own[head, 1] = jnp.dot(probs_low[1], g, preferred_element_type=F32)

    def finish(head):
        for which, factor in ((0, scale), (1, None)):
            for side in range(2):
                part_copy(head, which, side).wait_recv()
            summed = (
                own[head, which]
                + landed[head, which, 1].astype(F32)
                + landed[head, which, 0].astype(F32)
            )
            if factor is not None:
                summed = summed * factor
            results[head, 1 + which] = summed.astype(BF16)
            send_out(head, 1 + which)

    def await_rest(head):
        for which in range(2, 4):
            await_entry(head, which)
        for which in range(2):
            for side in range(2):
                band_arrival(head, which, side).wait_recv()

    send_band(0)
    mask_copy.wait()
    await_rest(0)
    send_band(1)
    compute(0)
    await_rest(1)
    finish(0)
    compute(1)
    finish(1)

    for head in range(HEADS_HERE):
        for which in range(4):
            for step in range(1, ulys):
                entry_copy(head, which, step).wait_send()
        for which in range(2):
            for side in range(2):
                band_copy(head, which, side).wait_send()
                part_copy(head, which, side).wait_send()
        for which in range(3):
            exit_local(head, which).wait()
            for step in range(1, ulys):
                exit_copy(head, which, step).wait_send()
                exit_arrival(head, which, step).wait_recv()


def local(cells, ulys, queries, keys, values, out_grad, block_mask):
    rows, width = queries.shape
    genes = rows * ulys
    n = HEADS_HERE
    dma = pltpu.SemaphoreType.DMA
    outputs = [jax.ShapeDtypeStruct((rows, width), BF16)] * 3
    return pl.pallas_call(
        functools.partial(kernel, cells, ulys),
        out_shape=outputs,
        in_specs=[pl.BlockSpec(memory_space=pl.ANY)] * 5,
        out_specs=[pl.BlockSpec(memory_space=pl.ANY)] * 3,
        scratch_shapes=[
            pltpu.VMEM((n, 2, 3, genes, DIM), BF16),
            pltpu.VMEM((n, 2, genes, DIM), BF16),
            pltpu.VMEM((3, genes, genes), F32),
            pltpu.VMEM((3, genes, genes), F32),
            pltpu.VMEM((3, genes, genes), BF16),
            pltpu.VMEM((3, genes, genes), BF16),
            pltpu.VMEM((n, 2, genes, DIM), F32),
            pltpu.VMEM((n, 2, 2, genes, DIM), BF16),
            pltpu.VMEM((n, 2, 2, genes, DIM), BF16),
            pltpu.VMEM((n, 3, genes, DIM), BF16),
            pltpu.SMEM((8, block_mask.shape[1]), jnp.int32),
            dma,
            dma((n, 4)),
            dma((n, 4, ulys - 1)),
            dma((n, 4, ulys - 1)),
            dma((n, 2, 2)),
            dma((n, 2, 2)),
            dma((n, 2, 2)),
            dma((n, 2, 2)),
            dma((n, 3)),
            dma((n, 3, ulys - 1)),
            dma((n, 3, ulys - 1)),
        ],
        compiler_params=pltpu.CompilerParams(
            collective_id=0, has_side_effects=True, vmem_limit_bytes=48 * 1024 * 1024
        ),
    )(queries, keys, values, out_grad, block_mask)


def solution(mesh):
    rows = P(("batch", "blk", "uly"), None)
    return jax.shard_map(
        functools.partial(local, mesh.shape["blk"], mesh.shape["uly"]),
        mesh=mesh,
        in_specs=(rows, rows, rows, rows, P("batch", None)),
        out_specs=(rows, rows, rows),
        check_vma=False,
    )
```

```python
import functools
import math

import jax
import jax.numpy as jnp
from jax import lax
from jax.experimental import pallas as pl
from jax.experimental.pallas import tpu as pltpu
from jax.sharding import PartitionSpec as P

MESH = pl.DeviceIdType.MESH
DIM = 128
BLOCK = 128
HEADS_HERE = 2
F32 = jnp.float32
BF16 = jnp.bfloat16


def times_t(left, right):
    return lax.dot_general(left, right, (((1,), (1,)), ((), ())), preferred_element_type=F32)


def groups_sum(block):
    rows, columns = block.shape
    return jnp.sum(block.reshape(rows // 8, 8, columns), axis=0)


def groups_max(block):
    rows, columns = block.shape
    return jnp.max(block.reshape(rows // 8, 8, columns), axis=0)


def kernel(
    cells,
    ulys,
    q_hbm,
    k_hbm,
    v_hbm,
    g_hbm,
    mask_hbm,
    dq_hbm,
    dk_hbm,
    dv_hbm,
    kv,
    qg,
    scores,
    dprobs,
    probs_low,
    dscores,
    own,
    sides,
    landed,
    results,
    mask,
    mask_sem,
    local_sem,
    in_send,
    in_recv,
    band_send,
    band_recv,
    part_send,
    part_recv,
    out_local,
    out_send,
    out_recv,
):
    b = lax.axis_index("blk")
    u = lax.axis_index("uly")
    rows = q_hbm.shape[0]
    genes = rows * ulys
    per_cell = genes // BLOCK
    half = cells // 2

    def group_of(blk, uly):
        upper = blk // half
        return uly + upper * (ulys - 1 - 2 * uly)

    prior = lax.rem(b + cells - 1, cells)
    following = lax.rem(b + 1, cells)
    my_group = group_of(b, u)
    prior_uly = group_of(prior, my_group)
    following_uly = group_of(following, my_group)
    sideways = (
        {"blk": prior, "uly": prior_uly},
        {"blk": following, "uly": following_uly},
    )

    def peer(step):
        return lax.rem(u + step, ulys)

    barrier = pltpu.get_barrier_semaphore()
    for step in range(1, ulys):
        pl.semaphore_signal(
            barrier, inc=1, device_id={"uly": peer(step)}, device_id_type=MESH
        )
    for side in sideways:
        pl.semaphore_signal(barrier, inc=1, device_id=side, device_id_type=MESH)

    mask_rows = (b * per_cell // 8) * 8
    mask_copy = pltpu.make_async_copy(
        mask_hbm.at[pl.ds(pl.multiple_of(mask_rows, 8), 8), :], mask, mask_sem
    )
    mask_copy.start()

    sources = (k_hbm, v_hbm, q_hbm, g_hbm)

    def landing(head, which, uly):
        at = pl.ds(pl.multiple_of(uly * rows, rows), rows)
        if which < 2:
            return kv.at[head, which, 1, at, :]
        return qg.at[head, which - 2, at, :]

    def columns_of(group, head):
        start = (group * HEADS_HERE + head) * DIM
        return pl.ds(pl.multiple_of(start, DIM), DIM)

    def entry_local(head, which):
        return pltpu.make_async_copy(
            sources[which].at[:, columns_of(my_group, head)],
            landing(head, which, u),
            local_sem.at[head, which],
        )

    def entry_copy(head, which, step):
        to = peer(step)
        return pltpu.make_async_remote_copy(
            src_ref=sources[which].at[:, columns_of(group_of(b, to), head)],
            dst_ref=landing(head, which, u),
            send_sem=in_send.at[head, which, step - 1],
            recv_sem=in_recv.at[head, which, step - 1],
            device_id={"uly": to},
            device_id_type=MESH,
        )

    def entry_arrival(head, which, step):
        came_from = lax.rem(u + ulys - step, ulys)
        return pltpu.make_async_remote_copy(
            src_ref=sources[which].at[:, columns_of(my_group, head)],
            dst_ref=landing(head, which, came_from),
            send_sem=in_send.at[head, which, step - 1],
            recv_sem=in_recv.at[head, which, step - 1],
            device_id={"uly": came_from},
            device_id_type=MESH,
        )

    for which in range(4):
        for head in range(HEADS_HERE):
            entry_local(head, which).start()

    pl.semaphore_wait(barrier, ulys + 1)

    for pair in ((0, 1), (2, 3)):
        for head in range(HEADS_HERE):
            for which in pair:
                for step in range(1, ulys):
                    entry_copy(head, which, step).start()

    def await_entry(head, which):
        entry_local(head, which).wait()
        for step in range(1, ulys):
            entry_arrival(head, which, step).wait_recv()

    def band_copy(head, which, side):
        return pltpu.make_async_remote_copy(
            src_ref=kv.at[head, which, 1],
            dst_ref=kv.at[head, which, 2 - 2 * side],
            send_sem=band_send.at[head, which, side],
            recv_sem=band_recv.at[head, which, side],
            device_id=sideways[side],
            device_id_type=MESH,
        )

    def band_arrival(head, which, side):
        return pltpu.make_async_remote_copy(
            src_ref=kv.at[head, which, 1],
            dst_ref=kv.at[head, which, 2 - 2 * side],
            send_sem=band_send.at[head, which, side],
            recv_sem=band_recv.at[head, which, side],
            device_id=sideways[side],
            device_id_type=MESH,
        )

    def send_band(head):
        for which in range(2):
            await_entry(head, which)
            for side in range(2):
                band_copy(head, which, side).start()

    def part_copy(head, which, side):
        return pltpu.make_async_remote_copy(
            src_ref=sides.at[head, which, side],
            dst_ref=landed.at[head, which, 1 - side],
            send_sem=part_send.at[head, which, side],
            recv_sem=part_recv.at[head, which, side],
            device_id=sideways[side],
            device_id_type=MESH,
        )

    outs = (dq_hbm, dk_hbm, dv_hbm)

    def exit_local(head, which):
        return pltpu.make_async_copy(
            results.at[head, which, pl.ds(pl.multiple_of(u * rows, rows), rows), :],
            outs[which].at[:, columns_of(my_group, head)],
            out_local.at[head, which],
        )

    def exit_copy(head, which, step):
        to = peer(step)
        return pltpu.make_async_remote_copy(
            src_ref=results.at[head, which, pl.ds(pl.multiple_of(to * rows, rows), rows), :],
            dst_ref=outs[which].at[:, columns_of(my_group, head)],
            send_sem=out_send.at[head, which, step - 1],
            recv_sem=out_recv.at[head, which, step - 1],
            device_id={"uly": to},
            device_id_type=MESH,
        )

    def exit_arrival(head, which, step):
        came_from = lax.rem(u + ulys - step, ulys)
        return pltpu.make_async_remote_copy(
            src_ref=results.at[head, which, pl.ds(0, rows), :],
            dst_ref=outs[which].at[:, columns_of(group_of(b, came_from), head)],
            send_sem=out_send.at[head, which, step - 1],
            recv_sem=out_recv.at[head, which, step - 1],
            device_id={"uly": came_from},
            device_id_type=MESH,
        )

    def send_out(head, which):
        exit_local(head, which).start()
        for step in range(1, ulys):
            exit_copy(head, which, step).start()

    scale = 1.0 / math.sqrt(DIM)
    scale2 = scale * math.log2(math.e)
    first_row = lax.rem(b * per_cell, 8)
    near = (prior, b, following)

    def bias_row(part, block):
        pieces = []
        for a in range(per_cell):
            allowed = mask[first_row + a, near[part] * per_cell + block] > 0
            pieces.append(jnp.full((1, BLOCK), jnp.where(allowed, 0.0, -1e30), F32))
        return jnp.concatenate(pieces, axis=1)

    parts = [(part, block) for part in range(3) for block in range(per_cell)]

    def compute(head):
        q = qg[head, 0]
        g = qg[head, 1]
        top = None
        for part, block in parts:
            at = slice(block * BLOCK, (block + 1) * BLOCK)
            s = times_t(kv[head, 0, part, at, :], q) * scale2 + bias_row(part, block)
            scores[part, at, :] = s
            here = groups_max(s)
            top = here if top is None else jnp.maximum(top, here)
            dprobs[part, at, :] = times_t(kv[head, 1, part, at, :], g)
        top = jnp.max(top, axis=0, keepdims=True)
        total = jnp.zeros((8, genes), F32)
        delta = jnp.zeros((8, genes), F32)
        for part, block in parts:
            at = slice(block * BLOCK, (block + 1) * BLOCK)
            e = jnp.exp2(scores[part, at, :] - top)
            scores[part, at, :] = e
            total += groups_sum(e)
            delta += groups_sum(e * dprobs[part, at, :])
        inverse = 1.0 / jnp.sum(total, axis=0, keepdims=True)
        delta = jnp.sum(delta, axis=0, keepdims=True) * inverse
        for part, block in parts:
            at = slice(block * BLOCK, (block + 1) * BLOCK)
            p = scores[part, at, :] * inverse
            probs_low[part, at, :] = p.astype(BF16)
            dscores[part, at, :] = (p * (dprobs[part, at, :] - delta)).astype(BF16)
        for side in range(2):
            sides[head, 0, side] = jnp.dot(
                dscores[2 * side], q, preferred_element_type=F32
            ).astype(BF16)
            part_copy(head, 0, side).start()
            sides[head, 1, side] = jnp.dot(
                probs_low[2 * side], g, preferred_element_type=F32
            ).astype(BF16)
            part_copy(head, 1, side).start()
        grad = jnp.zeros((DIM, genes), F32)
        for part in range(3):
            grad += jnp.dot(kv[head, 0, part].T, dscores[part], preferred_element_type=F32)
        results[head, 0] = (grad.T * scale).astype(BF16)
        own[head, 0] = jnp.dot(dscores[1], q, preferred_element_type=F32)
        own[head, 1] = jnp.dot(probs_low[1], g, preferred_element_type=F32)

    def finish(head):
        for which, factor in ((0, scale), (1, None)):
            for side in range(2):
                part_copy(head, which, side).wait_recv()
            summed = (
                own[head, which]
                + landed[head, which, 1].astype(F32)
                + landed[head, which, 0].astype(F32)
            )
            if factor is not None:
                summed = summed * factor
            results[head, 1 + which] = summed.astype(BF16)
            send_out(head, 1 + which)

    def await_rest(head):
        for which in range(2, 4):
            await_entry(head, which)
        for which in range(2):
            for side in range(2):
                band_arrival(head, which, side).wait_recv()

    mask_copy.wait()
    send_band(0)
    send_band(1)
    await_rest(0)
    compute(0)
    await_rest(1)
    send_out(0, 0)
    compute(1)
    send_out(1, 0)
    finish(0)
    finish(1)

    for head in range(HEADS_HERE):
        for which in range(4):
            for step in range(1, ulys):
                entry_copy(head, which, step).wait_send()
        for which in range(2):
            for side in range(2):
                band_copy(head, which, side).wait_send()
                part_copy(head, which, side).wait_send()
        for which in range(3):
            exit_local(head, which).wait()
            for step in range(1, ulys):
                exit_copy(head, which, step).wait_send()
                exit_arrival(head, which, step).wait_recv()


def settle(dq, dk, dv, dq_out, dk_out, dv_out, sems):
    pairs = ((dq, dq_out), (dk, dk_out), (dv, dv_out))
    copies = [pltpu.make_async_copy(*pair, sems.at[i]) for i, pair in enumerate(pairs)]
    for copy in copies:
        copy.start()
    for copy in copies:
        copy.wait()


def local(cells, ulys, queries, keys, values, out_grad, block_mask):
    rows, width = queries.shape
    genes = rows * ulys
    n = HEADS_HERE
    dma = pltpu.SemaphoreType.DMA
    outputs = [jax.ShapeDtypeStruct((rows, width), BF16)] * 3
    grads = pl.pallas_call(
        functools.partial(kernel, cells, ulys),
        out_shape=outputs,
        in_specs=[pl.BlockSpec(memory_space=pltpu.HBM)] * 5,
        out_specs=[pl.BlockSpec(memory_space=pl.ANY)] * 3,
        scratch_shapes=[
            pltpu.VMEM((n, 2, 3, genes, DIM), BF16),
            pltpu.VMEM((n, 2, genes, DIM), BF16),
            pltpu.VMEM((3, genes, genes), F32),
            pltpu.VMEM((3, genes, genes), F32),
            pltpu.VMEM((3, genes, genes), BF16),
            pltpu.VMEM((3, genes, genes), BF16),
            pltpu.VMEM((n, 2, genes, DIM), F32),
            pltpu.VMEM((n, 2, 2, genes, DIM), BF16),
            pltpu.VMEM((n, 2, 2, genes, DIM), BF16),
            pltpu.VMEM((n, 3, genes, DIM), BF16),
            pltpu.SMEM((8, block_mask.shape[1]), jnp.int32),
            dma,
            dma((n, 4)),
            dma((n, 4, ulys - 1)),
            dma((n, 4, ulys - 1)),
            dma((n, 2, 2)),
            dma((n, 2, 2)),
            dma((n, 2, 2)),
            dma((n, 2, 2)),
            dma((n, 3)),
            dma((n, 3, ulys - 1)),
            dma((n, 3, ulys - 1)),
        ],
        compiler_params=pltpu.CompilerParams(
            collective_id=0, has_side_effects=True, vmem_limit_bytes=40 * 1024 * 1024
        ),
    )(*(pltpu.with_memory_space_constraint(x, pltpu.HBM) for x in (queries, keys, values, out_grad, block_mask)))
    return pl.pallas_call(
        settle,
        out_shape=outputs,
        in_specs=[pl.BlockSpec(memory_space=pl.ANY)] * 3,
        out_specs=[pl.BlockSpec(memory_space=pltpu.HBM)] * 3,
        scratch_shapes=[dma((3,))],
        compiler_params=pltpu.CompilerParams(vmem_limit_bytes=1024 * 1024),
    )(*grads)


def solution(mesh):
    rows = P(("batch", "blk", "uly"), None)
    return jax.shard_map(
        functools.partial(local, mesh.shape["blk"], mesh.shape["uly"]),
        mesh=mesh,
        in_specs=(rows, rows, rows, rows, P("batch", None)),
        out_specs=(rows, rows, rows),
        check_vma=False,
    )
```

```python
import functools
import math

import jax
import jax.numpy as jnp
from jax import lax
from jax.experimental import pallas as pl
from jax.experimental.pallas import tpu as pltpu
from jax.sharding import PartitionSpec as P

MESH = pl.DeviceIdType.MESH
DIM = 128
BLOCK = 128
HEADS_HERE = 2
F32 = jnp.float32
BF16 = jnp.bfloat16


def times_t(left, right):
    return lax.dot_general(left, right, (((1,), (1,)), ((), ())), preferred_element_type=F32)


def groups_sum(block):
    rows, columns = block.shape
    return jnp.sum(block.reshape(rows // 8, 8, columns), axis=0)


def groups_max(block):
    rows, columns = block.shape
    return jnp.max(block.reshape(rows // 8, 8, columns), axis=0)


def kernel(
    cells,
    ulys,
    q_hbm,
    k_hbm,
    v_hbm,
    g_hbm,
    mask_hbm,
    dq_hbm,
    dk_hbm,
    dv_hbm,
    kv,
    qg,
    scores,
    dprobs,
    probs_low,
    dscores,
    own,
    sides,
    landed,
    results,
    mask,
    mask_sem,
    ready,
    ready_side,
    local_sem,
    in_send,
    in_recv,
    band_send,
    band_recv,
    part_send,
    part_recv,
    out_local,
    out_send,
    out_recv,
):
    b = lax.axis_index("blk")
    u = lax.axis_index("uly")
    rows = q_hbm.shape[0]
    genes = rows * ulys
    per_cell = genes // BLOCK
    half = cells // 2

    def group_of(blk, uly):
        upper = blk // half
        return uly + upper * (ulys - 1 - 2 * uly)

    prior = lax.rem(b + cells - 1, cells)
    following = lax.rem(b + 1, cells)
    my_group = group_of(b, u)
    prior_uly = group_of(prior, my_group)
    following_uly = group_of(following, my_group)
    sideways = (
        {"blk": prior, "uly": prior_uly},
        {"blk": following, "uly": following_uly},
    )

    def peer(step):
        return lax.rem(u + step, ulys)

    listens = lax.rem(b + 1, 2)
    barrier = pltpu.get_barrier_semaphore()
    for step in range(1, ulys):
        to = peer(step)

        @pl.when((to < u) | ((u == ulys - 2) & (to == ulys - 1)))
        def _():
            pl.semaphore_signal(barrier, inc=1, device_id={"uly": to}, device_id_type=MESH)

    @pl.when(listens == 0)
    def _():
        for side in sideways:
            pl.semaphore_signal(barrier, inc=1, device_id=side, device_id_type=MESH)

    mask_rows = (b * per_cell // 8) * 8
    mask_copy = pltpu.make_async_copy(
        mask_hbm.at[pl.ds(pl.multiple_of(mask_rows, 8), 8), :], mask, mask_sem
    )
    mask_copy.start()

    sources = (k_hbm, v_hbm, q_hbm, g_hbm)

    def landing(head, which, uly):
        at = pl.ds(pl.multiple_of(uly * rows, rows), rows)
        if which < 2:
            return kv.at[head, which, 1, at, :]
        return qg.at[head, which - 2, at, :]

    def columns_of(group, head):
        start = (group * HEADS_HERE + head) * DIM
        return pl.ds(pl.multiple_of(start, DIM), DIM)

    def entry_local(head, which):
        return pltpu.make_async_copy(
            sources[which].at[:, columns_of(my_group, head)],
            landing(head, which, u),
            local_sem.at[head, which],
        )

    def entry_copy(head, which, step):
        to = peer(step)
        return pltpu.make_async_remote_copy(
            src_ref=sources[which].at[:, columns_of(group_of(b, to), head)],
            dst_ref=landing(head, which, u),
            send_sem=in_send.at[head, which, step - 1],
            recv_sem=in_recv.at[head, which, step - 1],
            device_id={"uly": to},
            device_id_type=MESH,
        )

    def entry_arrival(head, which, step):
        came_from = lax.rem(u + ulys - step, ulys)
        return pltpu.make_async_remote_copy(
            src_ref=sources[which].at[:, columns_of(my_group, head)],
            dst_ref=landing(head, which, came_from),
            send_sem=in_send.at[head, which, step - 1],
            recv_sem=in_recv.at[head, which, step - 1],
            device_id={"uly": came_from},
            device_id_type=MESH,
        )

    for which in range(4):
        for head in range(HEADS_HERE):
            entry_local(head, which).start()

    pl.semaphore_wait(barrier, jnp.where(u == ulys - 1, 1, ulys - 1 - u) + 2 * listens)
    for step in range(1, ulys):
        to = peer(step)

        @pl.when(to > u)
        def _():
            pl.semaphore_signal(
                ready.at[step - 1], inc=1, device_id={"uly": to}, device_id_type=MESH
            )

    @pl.when(listens == 1)
    def _():
        for side in range(2):
            pl.semaphore_signal(
                ready_side.at[1 - side], inc=1, device_id=sideways[side], device_id_type=MESH
            )

    for last in (False, True):
        for step in range(1, ulys):
            to = peer(step)

            @pl.when((to < u) & ((to == 0) == last))
            def _():
                pl.semaphore_wait(ready.at[ulys - 1 - step], 1)

        for head in range(HEADS_HERE):
            for which in range(2):
                for step in range(1, ulys):

                    @pl.when((peer(step) == 0) == last)
                    def _():
                        entry_copy(head, which, step).start()

    for head in range(HEADS_HERE):
        for which in range(2, 4):
            for step in range(1, ulys):
                entry_copy(head, which, step).start()

    def await_entry(head, which):
        entry_local(head, which).wait()
        for step in range(1, ulys):
            entry_arrival(head, which, step).wait_recv()

    def band_copy(head, which, side):
        return pltpu.make_async_remote_copy(
            src_ref=kv.at[head, which, 1],
            dst_ref=kv.at[head, which, 2 - 2 * side],
            send_sem=band_send.at[head, which, side],
            recv_sem=band_recv.at[head, which, side],
            device_id=sideways[side],
            device_id_type=MESH,
        )

    def band_arrival(head, which, side):
        return pltpu.make_async_remote_copy(
            src_ref=kv.at[head, which, 1],
            dst_ref=kv.at[head, which, 2 - 2 * side],
            send_sem=band_send.at[head, which, side],
            recv_sem=band_recv.at[head, which, side],
            device_id=sideways[side],
            device_id_type=MESH,
        )

    def send_band(head):
        for which in range(2):
            await_entry(head, which)
            for side in range(2):
                band_copy(head, which, side).start()

    def part_copy(head, which, side):
        return pltpu.make_async_remote_copy(
            src_ref=sides.at[head, which, side],
            dst_ref=landed.at[head, which, 1 - side],
            send_sem=part_send.at[head, which, side],
            recv_sem=part_recv.at[head, which, side],
            device_id=sideways[side],
            device_id_type=MESH,
        )

    outs = (dq_hbm, dk_hbm, dv_hbm)

    def exit_local(head, which):
        return pltpu.make_async_copy(
            results.at[head, which, pl.ds(pl.multiple_of(u * rows, rows), rows), :],
            outs[which].at[:, columns_of(my_group, head)],
            out_local.at[head, which],
        )

    def exit_copy(head, which, step):
        to = peer(step)
        return pltpu.make_async_remote_copy(
            src_ref=results.at[head, which, pl.ds(pl.multiple_of(to * rows, rows), rows), :],
            dst_ref=outs[which].at[:, columns_of(my_group, head)],
            send_sem=out_send.at[head, which, step - 1],
            recv_sem=out_recv.at[head, which, step - 1],
            device_id={"uly": to},
            device_id_type=MESH,
        )

    def exit_arrival(head, which, step):
        came_from = lax.rem(u + ulys - step, ulys)
        return pltpu.make_async_remote_copy(
            src_ref=results.at[head, which, pl.ds(0, rows), :],
            dst_ref=outs[which].at[:, columns_of(group_of(b, came_from), head)],
            send_sem=out_send.at[head, which, step - 1],
            recv_sem=out_recv.at[head, which, step - 1],
            device_id={"uly": came_from},
            device_id_type=MESH,
        )

    def send_out(head, which):
        exit_local(head, which).start()
        for step in range(1, ulys):
            exit_copy(head, which, step).start()

    scale = 1.0 / math.sqrt(DIM)
    scale2 = scale * math.log2(math.e)
    first_row = lax.rem(b * per_cell, 8)
    near = (prior, b, following)

    def bias_row(part, block):
        pieces = []
        for a in range(per_cell):
            allowed = mask[first_row + a, near[part] * per_cell + block] > 0
            pieces.append(jnp.full((1, BLOCK), jnp.where(allowed, 0.0, -1e30), F32))
        return jnp.concatenate(pieces, axis=1)

    parts = [(part, block) for part in range(3) for block in range(per_cell)]

    def compute(head):
        q = qg[head, 0]
        g = qg[head, 1]
        top = None
        for part, block in parts:
            at = slice(block * BLOCK, (block + 1) * BLOCK)
            s = times_t(kv[head, 0, part, at, :], q) * scale2 + bias_row(part, block)
            scores[part, at, :] = s
            here = groups_max(s)
            top = here if top is None else jnp.maximum(top, here)
            dprobs[part, at, :] = times_t(kv[head, 1, part, at, :], g)
        top = jnp.max(top, axis=0, keepdims=True)
        total = jnp.zeros((8, genes), F32)
        delta = jnp.zeros((8, genes), F32)
        for part, block in parts:
            at = slice(block * BLOCK, (block + 1) * BLOCK)
            e = jnp.exp2(scores[part, at, :] - top)
            scores[part, at, :] = e
            total += groups_sum(e)
            delta += groups_sum(e * dprobs[part, at, :])
        inverse = 1.0 / jnp.sum(total, axis=0, keepdims=True)
        delta = jnp.sum(delta, axis=0, keepdims=True) * inverse
        for part, block in parts:
            at = slice(block * BLOCK, (block + 1) * BLOCK)
            p = scores[part, at, :] * inverse
            probs_low[part, at, :] = p.astype(BF16)
            dscores[part, at, :] = (p * (dprobs[part, at, :] - delta)).astype(BF16)
        for side in range(2):
            sides[head, 0, side] = jnp.dot(
                dscores[2 * side], q, preferred_element_type=F32
            ).astype(BF16)
            part_copy(head, 0, side).start()
            sides[head, 1, side] = jnp.dot(
                probs_low[2 * side], g, preferred_element_type=F32
            ).astype(BF16)
            part_copy(head, 1, side).start()
        grad = jnp.zeros((DIM, genes), F32)
        for part in range(3):
            grad += jnp.dot(kv[head, 0, part].T, dscores[part], preferred_element_type=F32)
        results[head, 0] = (grad.T * scale).astype(BF16)
        own[head, 0] = jnp.dot(dscores[1], q, preferred_element_type=F32)
        own[head, 1] = jnp.dot(probs_low[1], g, preferred_element_type=F32)

    def finish(head):
        for which, factor in ((0, scale), (1, None)):
            for side in range(2):
                part_copy(head, which, side).wait_recv()
            summed = (
                own[head, which]
                + landed[head, which, 1].astype(F32)
                + landed[head, which, 0].astype(F32)
            )
            if factor is not None:
                summed = summed * factor
            results[head, 1 + which] = summed.astype(BF16)
            send_out(head, 1 + which)

    def await_rest(head):
        for which in range(2, 4):
            await_entry(head, which)
        for which in range(2):
            for side in range(2):
                band_arrival(head, which, side).wait_recv()

    mask_copy.wait()

    @pl.when(listens == 0)
    def _():
        for side in range(2):
            pl.semaphore_wait(ready_side.at[side], 1)

    send_band(0)
    send_band(1)
    await_rest(0)
    compute(0)
    await_rest(1)
    send_out(0, 0)
    compute(1)
    send_out(1, 0)
    finish(0)
    finish(1)

    for head in range(HEADS_HERE):
        for which in range(4):
            for step in range(1, ulys):
                entry_copy(head, which, step).wait_send()
        for which in range(2):
            for side in range(2):
                band_copy(head, which, side).wait_send()
                part_copy(head, which, side).wait_send()
        for which in range(3):
            exit_local(head, which).wait()
            for step in range(1, ulys):
                exit_copy(head, which, step).wait_send()
                exit_arrival(head, which, step).wait_recv()


def settle(dq, dk, dv, dq_out, dk_out, dv_out, sems):
    pairs = ((dq, dq_out), (dk, dk_out), (dv, dv_out))
    copies = [pltpu.make_async_copy(*pair, sems.at[i]) for i, pair in enumerate(pairs)]
    for copy in copies:
        copy.start()
    for copy in copies:
        copy.wait()


def local(cells, ulys, queries, keys, values, out_grad, block_mask):
    rows, width = queries.shape
    genes = rows * ulys
    n = HEADS_HERE
    dma = pltpu.SemaphoreType.DMA
    outputs = [jax.ShapeDtypeStruct((rows, width), BF16)] * 3
    grads = pl.pallas_call(
        functools.partial(kernel, cells, ulys),
        out_shape=outputs,
        in_specs=[pl.BlockSpec(memory_space=pltpu.HBM)] * 5,
        out_specs=[pl.BlockSpec(memory_space=pl.ANY)] * 3,
        scratch_shapes=[
            pltpu.VMEM((n, 2, 3, genes, DIM), BF16),
            pltpu.VMEM((n, 2, genes, DIM), BF16),
            pltpu.VMEM((3, genes, genes), F32),
            pltpu.VMEM((3, genes, genes), F32),
            pltpu.VMEM((3, genes, genes), BF16),
            pltpu.VMEM((3, genes, genes), BF16),
            pltpu.VMEM((n, 2, genes, DIM), F32),
            pltpu.VMEM((n, 2, 2, genes, DIM), BF16),
            pltpu.VMEM((n, 2, 2, genes, DIM), BF16),
            pltpu.VMEM((n, 3, genes, DIM), BF16),
            pltpu.SMEM((8, block_mask.shape[1]), jnp.int32),
            dma,
            pltpu.SemaphoreType.REGULAR((ulys - 1,)),
            pltpu.SemaphoreType.REGULAR((2,)),
            dma((n, 4)),
            dma((n, 4, ulys - 1)),
            dma((n, 4, ulys - 1)),
            dma((n, 2, 2)),
            dma((n, 2, 2)),
            dma((n, 2, 2)),
            dma((n, 2, 2)),
            dma((n, 3)),
            dma((n, 3, ulys - 1)),
            dma((n, 3, ulys - 1)),
        ],
        compiler_params=pltpu.CompilerParams(
            collective_id=0, has_side_effects=True, vmem_limit_bytes=40 * 1024 * 1024
        ),
    )(*(pltpu.with_memory_space_constraint(x, pltpu.HBM) for x in (queries, keys, values, out_grad, block_mask)))
    return pl.pallas_call(
        settle,
        out_shape=outputs,
        in_specs=[pl.BlockSpec(memory_space=pl.ANY)] * 3,
        out_specs=[pl.BlockSpec(memory_space=pltpu.HBM)] * 3,
        scratch_shapes=[dma((3,))],
        compiler_params=pltpu.CompilerParams(vmem_limit_bytes=1024 * 1024),
    )(*grads)


def solution(mesh):
    rows = P(("batch", "blk", "uly"), None)
    return jax.shard_map(
        functools.partial(local, mesh.shape["blk"], mesh.shape["uly"]),
        mesh=mesh,
        in_specs=(rows, rows, rows, rows, P("batch", None)),
        out_specs=(rows, rows, rows),
        check_vma=False,
    )
```

```python
import functools
import math

import jax
import jax.numpy as jnp
from jax import lax
from jax.experimental import pallas as pl
from jax.experimental.pallas import tpu as pltpu
from jax.sharding import PartitionSpec as P

MESH = pl.DeviceIdType.MESH
DIM = 128
BLOCK = 128
HEADS_HERE = 2
F32 = jnp.float32
BF16 = jnp.bfloat16


def times_t(left, right):
    return lax.dot_general(left, right, (((1,), (1,)), ((), ())), preferred_element_type=F32)


def groups_sum(block):
    rows, columns = block.shape
    return jnp.sum(block.reshape(rows // 8, 8, columns), axis=0)


def groups_max(block):
    rows, columns = block.shape
    return jnp.max(block.reshape(rows // 8, 8, columns), axis=0)


def kernel(
    cells,
    ulys,
    q_hbm,
    k_hbm,
    v_hbm,
    g_hbm,
    mask_hbm,
    dq_hbm,
    dk_hbm,
    dv_hbm,
    kv,
    qg,
    scores,
    dprobs,
    probs_low,
    dscores,
    own,
    sides,
    landed,
    results,
    mask,
    mask_sem,
    ready,
    ready_side,
    local_sem,
    in_send,
    in_recv,
    band_send,
    band_recv,
    part_send,
    part_recv,
    out_local,
    out_send,
    out_recv,
):
    b = lax.axis_index("blk")
    u = lax.axis_index("uly")
    rows = q_hbm.shape[0]
    genes = rows * ulys
    per_cell = genes // BLOCK
    half = cells // 2

    def group_of(blk, uly):
        upper = blk // half
        return uly + upper * (ulys - 1 - 2 * uly)

    prior = lax.rem(b + cells - 1, cells)
    following = lax.rem(b + 1, cells)
    my_group = group_of(b, u)
    prior_uly = group_of(prior, my_group)
    following_uly = group_of(following, my_group)
    sideways = (
        {"blk": prior, "uly": prior_uly},
        {"blk": following, "uly": following_uly},
    )

    def peer(step):
        return lax.rem(u + step, ulys)

    listens = lax.rem(b + 1, 2)
    barrier = pltpu.get_barrier_semaphore()
    for step in range(1, ulys):
        to = peer(step)

        @pl.when((to < u) | ((u == ulys - 2) & (to == ulys - 1)))
        def _():
            pl.semaphore_signal(barrier, inc=1, device_id={"uly": to}, device_id_type=MESH)

    @pl.when(listens == 0)
    def _():
        for side in sideways:
            pl.semaphore_signal(barrier, inc=1, device_id=side, device_id_type=MESH)

    mask_rows = (b * per_cell // 8) * 8
    mask_copy = pltpu.make_async_copy(
        mask_hbm.at[pl.ds(pl.multiple_of(mask_rows, 8), 8), :], mask, mask_sem
    )
    mask_copy.start()

    sources = (k_hbm, v_hbm, q_hbm, g_hbm)

    def landing(head, which, uly):
        at = pl.ds(pl.multiple_of(uly * rows, rows), rows)
        if which < 2:
            return kv.at[head, which, 1, at, :]
        return qg.at[head, which - 2, at, :]

    def columns_of(group, head):
        start = (group * HEADS_HERE + head) * DIM
        return pl.ds(pl.multiple_of(start, DIM), DIM)

    def entry_local(head, which):
        return pltpu.make_async_copy(
            sources[which].at[:, columns_of(my_group, head)],
            landing(head, which, u),
            local_sem.at[head, which],
        )

    def entry_copy(head, which, step):
        to = peer(step)
        return pltpu.make_async_remote_copy(
            src_ref=sources[which].at[:, columns_of(group_of(b, to), head)],
            dst_ref=landing(head, which, u),
            send_sem=in_send.at[head, which, step - 1],
            recv_sem=in_recv.at[head, which, step - 1],
            device_id={"uly": to},
            device_id_type=MESH,
        )

    def entry_arrival(head, which, step):
        came_from = lax.rem(u + ulys - step, ulys)
        return pltpu.make_async_remote_copy(
            src_ref=sources[which].at[:, columns_of(my_group, head)],
            dst_ref=landing(head, which, came_from),
            send_sem=in_send.at[head, which, step - 1],
            recv_sem=in_recv.at[head, which, step - 1],
            device_id={"uly": came_from},
            device_id_type=MESH,
        )

    for which in range(4):
        for head in range(HEADS_HERE):
            entry_local(head, which).start()

    pl.semaphore_wait(barrier, jnp.where(u == ulys - 1, 1, ulys - 1 - u) + 2 * listens)
    for step in range(1, ulys):
        to = peer(step)

        @pl.when(to > u)
        def _():
            pl.semaphore_signal(
                ready.at[step - 1], inc=1, device_id={"uly": to}, device_id_type=MESH
            )

    @pl.when(listens == 1)
    def _():
        for side in range(2):
            pl.semaphore_signal(
                ready_side.at[1 - side], inc=1, device_id=sideways[side], device_id_type=MESH
            )

    for last in (False, True):
        for step in range(1, ulys):
            to = peer(step)

            @pl.when((to < u) & ((to == 0) == last))
            def _():
                pl.semaphore_wait(ready.at[ulys - 1 - step], 1)

        for head in range(HEADS_HERE):
            for which in range(2):
                for step in range(1, ulys):

                    @pl.when((peer(step) == 0) == last)
                    def _():
                        entry_copy(head, which, step).start()

    def start_rest(head):
        for which in range(2, 4):
            for step in range(1, ulys):
                entry_copy(head, which, step).start()

    def await_entry(head, which):
        entry_local(head, which).wait()
        for step in range(1, ulys):
            entry_arrival(head, which, step).wait_recv()

    def band_copy(head, which, side):
        return pltpu.make_async_remote_copy(
            src_ref=kv.at[head, which, 1],
            dst_ref=kv.at[head, which, 2 - 2 * side],
            send_sem=band_send.at[head, which, side],
            recv_sem=band_recv.at[head, which, side],
            device_id=sideways[side],
            device_id_type=MESH,
        )

    def band_arrival(head, which, side):
        return pltpu.make_async_remote_copy(
            src_ref=kv.at[head, which, 1],
            dst_ref=kv.at[head, which, 2 - 2 * side],
            send_sem=band_send.at[head, which, side],
            recv_sem=band_recv.at[head, which, side],
            device_id=sideways[side],
            device_id_type=MESH,
        )

    def send_band(head):
        for which in range(2):
            for side in range(2):
                band_copy(head, which, side).start()

    def part_copy(head, which, side):
        return pltpu.make_async_remote_copy(
            src_ref=sides.at[head, which, side],
            dst_ref=landed.at[head, which, 1 - side],
            send_sem=part_send.at[head, which, side],
            recv_sem=part_recv.at[head, which, side],
            device_id=sideways[side],
            device_id_type=MESH,
        )

    outs = (dq_hbm, dk_hbm, dv_hbm)

    def exit_local(head, which):
        return pltpu.make_async_copy(
            results.at[head, which, pl.ds(pl.multiple_of(u * rows, rows), rows), :],
            outs[which].at[:, columns_of(my_group, head)],
            out_local.at[head, which],
        )

    def exit_copy(head, which, step):
        to = peer(step)
        return pltpu.make_async_remote_copy(
            src_ref=results.at[head, which, pl.ds(pl.multiple_of(to * rows, rows), rows), :],
            dst_ref=outs[which].at[:, columns_of(my_group, head)],
            send_sem=out_send.at[head, which, step - 1],
            recv_sem=out_recv.at[head, which, step - 1],
            device_id={"uly": to},
            device_id_type=MESH,
        )

    def exit_arrival(head, which, step):
        came_from = lax.rem(u + ulys - step, ulys)
        return pltpu.make_async_remote_copy(
            src_ref=results.at[head, which, pl.ds(0, rows), :],
            dst_ref=outs[which].at[:, columns_of(group_of(b, came_from), head)],
            send_sem=out_send.at[head, which, step - 1],
            recv_sem=out_recv.at[head, which, step - 1],
            device_id={"uly": came_from},
            device_id_type=MESH,
        )

    def send_out(head, which):
        exit_local(head, which).start()
        for step in range(1, ulys):
            exit_copy(head, which, step).start()

    scale = 1.0 / math.sqrt(DIM)
    scale2 = scale * math.log2(math.e)
    first_row = lax.rem(b * per_cell, 8)
    near = (prior, b, following)

    def bias_row(part, block):
        pieces = []
        for a in range(per_cell):
            allowed = mask[first_row + a, near[part] * per_cell + block] > 0
            pieces.append(jnp.full((1, BLOCK), jnp.where(allowed, 0.0, -1e30), F32))
        return jnp.concatenate(pieces, axis=1)

    parts = [(part, block) for part in range(3) for block in range(per_cell)]

    def block_rows(block):
        return slice(block * BLOCK, (block + 1) * BLOCK)

    def softmax(head):
        q = qg[head, 0]
        top = None
        for part, block in parts:
            at = block_rows(block)
            s = times_t(kv[head, 0, part, at, :], q) * scale2 + bias_row(part, block)
            scores[head, part, at, :] = s
            here = groups_max(s)
            top = here if top is None else jnp.maximum(top, here)
        top = jnp.max(top, axis=0, keepdims=True)
        total = jnp.zeros((8, genes), F32)
        for part, block in parts:
            at = block_rows(block)
            e = jnp.exp2(scores[head, part, at, :] - top)
            scores[head, part, at, :] = e
            total += groups_sum(e)
        inverse = 1.0 / jnp.sum(total, axis=0, keepdims=True)
        for part, block in parts:
            at = block_rows(block)
            probs_low[head, part, at, :] = (scores[head, part, at, :] * inverse).astype(BF16)
        return inverse

    def gradients(head, inverse):
        q = qg[head, 0]
        g = qg[head, 1]
        for side in range(2):
            sides[head, 1, side] = jnp.dot(
                probs_low[head, 2 * side], g, preferred_element_type=F32
            ).astype(BF16)
            part_copy(head, 1, side).start()
        delta = jnp.zeros((8, genes), F32)
        for part, block in parts:
            at = block_rows(block)
            d = times_t(kv[head, 1, part, at, :], g)
            dprobs[part, at, :] = d
            delta += groups_sum(scores[head, part, at, :] * d)
        delta = jnp.sum(delta, axis=0, keepdims=True) * inverse
        for part, block in parts:
            at = block_rows(block)
            p = scores[head, part, at, :] * inverse
            dscores[part, at, :] = (p * (dprobs[part, at, :] - delta)).astype(BF16)
        for side in range(2):
            sides[head, 0, side] = jnp.dot(
                dscores[2 * side], q, preferred_element_type=F32
            ).astype(BF16)
            part_copy(head, 0, side).start()
        grad = jnp.zeros((DIM, genes), F32)
        for part in range(3):
            grad += jnp.dot(kv[head, 0, part].T, dscores[part], preferred_element_type=F32)
        results[head, 0] = (grad.T * scale).astype(BF16)
        own[head, 1] = jnp.dot(probs_low[head, 1], g, preferred_element_type=F32)
        own[head, 0] = jnp.dot(dscores[1], q, preferred_element_type=F32)

    def finish(head):
        for which, factor in ((1, None), (0, scale)):
            for side in range(2):
                part_copy(head, which, side).wait_recv()
            summed = (
                own[head, which]
                + landed[head, which, 1].astype(F32)
                + landed[head, which, 0].astype(F32)
            )
            if factor is not None:
                summed = summed * factor
            results[head, 1 + which] = summed.astype(BF16)
            send_out(head, 1 + which)

    def await_band(head, which):
        for side in range(2):
            band_arrival(head, which, side).wait_recv()

    mask_copy.wait()

    for which in range(2):
        await_entry(0, which)
    start_rest(0)

    @pl.when(listens == 0)
    def _():
        for side in range(2):
            pl.semaphore_wait(ready_side.at[side], 1)

    send_band(0)
    for which in range(2):
        await_entry(1, which)
    start_rest(1)
    send_band(1)
    await_entry(0, 2)
    await_band(0, 0)
    inverse = softmax(0)
    await_entry(0, 3)
    await_band(0, 1)
    gradients(0, inverse)
    await_entry(1, 2)
    await_band(1, 0)
    inverse = softmax(1)
    await_entry(1, 3)
    send_out(0, 0)
    await_band(1, 1)
    gradients(1, inverse)
    send_out(1, 0)
    finish(0)
    finish(1)

    for head in range(HEADS_HERE):
        for which in range(4):
            for step in range(1, ulys):
                entry_copy(head, which, step).wait_send()
        for which in range(2):
            for side in range(2):
                band_copy(head, which, side).wait_send()
                part_copy(head, which, side).wait_send()
        for which in range(3):
            exit_local(head, which).wait()
            for step in range(1, ulys):
                exit_copy(head, which, step).wait_send()
                exit_arrival(head, which, step).wait_recv()


def settle(dq, dk, dv, dq_out, dk_out, dv_out, sems):
    pairs = ((dq, dq_out), (dk, dk_out), (dv, dv_out))
    copies = [pltpu.make_async_copy(*pair, sems.at[i]) for i, pair in enumerate(pairs)]
    for copy in copies:
        copy.start()
    for copy in copies:
        copy.wait()


def local(cells, ulys, queries, keys, values, out_grad, block_mask):
    rows, width = queries.shape
    genes = rows * ulys
    n = HEADS_HERE
    dma = pltpu.SemaphoreType.DMA
    outputs = [jax.ShapeDtypeStruct((rows, width), BF16)] * 3
    grads = pl.pallas_call(
        functools.partial(kernel, cells, ulys),
        out_shape=outputs,
        in_specs=[pl.BlockSpec(memory_space=pltpu.HBM)] * 5,
        out_specs=[pl.BlockSpec(memory_space=pl.ANY)] * 3,
        scratch_shapes=[
            pltpu.VMEM((n, 2, 3, genes, DIM), BF16),
            pltpu.VMEM((n, 2, genes, DIM), BF16),
            pltpu.VMEM((n, 3, genes, genes), F32),
            pltpu.VMEM((3, genes, genes), F32),
            pltpu.VMEM((n, 3, genes, genes), BF16),
            pltpu.VMEM((3, genes, genes), BF16),
            pltpu.VMEM((n, 2, genes, DIM), F32),
            pltpu.VMEM((n, 2, 2, genes, DIM), BF16),
            pltpu.VMEM((n, 2, 2, genes, DIM), BF16),
            pltpu.VMEM((n, 3, genes, DIM), BF16),
            pltpu.SMEM((8, block_mask.shape[1]), jnp.int32),
            dma,
            pltpu.SemaphoreType.REGULAR((ulys - 1,)),
            pltpu.SemaphoreType.REGULAR((2,)),
            dma((n, 4)),
            dma((n, 4, ulys - 1)),
            dma((n, 4, ulys - 1)),
            dma((n, 2, 2)),
            dma((n, 2, 2)),
            dma((n, 2, 2)),
            dma((n, 2, 2)),
            dma((n, 3)),
            dma((n, 3, ulys - 1)),
            dma((n, 3, ulys - 1)),
        ],
        compiler_params=pltpu.CompilerParams(
            collective_id=0, has_side_effects=True, vmem_limit_bytes=40 * 1024 * 1024
        ),
    )(*(pltpu.with_memory_space_constraint(x, pltpu.HBM) for x in (queries, keys, values, out_grad, block_mask)))
    return pl.pallas_call(
        settle,
        out_shape=outputs,
        in_specs=[pl.BlockSpec(memory_space=pl.ANY)] * 3,
        out_specs=[pl.BlockSpec(memory_space=pltpu.HBM)] * 3,
        scratch_shapes=[dma((3,))],
        compiler_params=pltpu.CompilerParams(vmem_limit_bytes=1024 * 1024),
    )(*grads)


def solution(mesh):
    rows = P(("batch", "blk", "uly"), None)
    return jax.shard_map(
        functools.partial(local, mesh.shape["blk"], mesh.shape["uly"]),
        mesh=mesh,
        in_specs=(rows, rows, rows, rows, P("batch", None)),
        out_specs=(rows, rows, rows),
        check_vma=False,
    )
```

```python
import functools
import math

import jax
import jax.numpy as jnp
from jax import lax
from jax.experimental import pallas as pl
from jax.experimental.pallas import tpu as pltpu
from jax.sharding import PartitionSpec as P

MESH = pl.DeviceIdType.MESH
DIM = 128
BLOCK = 128
HEADS_HERE = 2
F32 = jnp.float32
BF16 = jnp.bfloat16


def times_t(left, right):
    return lax.dot_general(left, right, (((1,), (1,)), ((), ())), preferred_element_type=F32)


def groups_sum(block):
    rows, columns = block.shape
    return jnp.sum(block.reshape(rows // 8, 8, columns), axis=0)


def groups_max(block):
    rows, columns = block.shape
    return jnp.max(block.reshape(rows // 8, 8, columns), axis=0)


def kernel(
    cells,
    ulys,
    q_hbm,
    k_hbm,
    v_hbm,
    g_hbm,
    mask_hbm,
    dq_hbm,
    dk_hbm,
    dv_hbm,
    kv,
    qg,
    scores,
    dprobs,
    probs_low,
    dscores,
    own,
    sides,
    landed,
    results,
    mask,
    mask_sem,
    ready,
    ready_side,
    local_sem,
    in_send,
    in_recv,
    band_send,
    band_recv,
    part_send,
    part_recv,
    out_local,
    out_send,
    out_recv,
):
    b = lax.axis_index("blk")
    u = lax.axis_index("uly")
    rows = q_hbm.shape[0]
    genes = rows * ulys
    per_cell = genes // BLOCK
    half = cells // 2

    def group_of(blk, uly):
        upper = blk // half
        return uly + upper * (ulys - 1 - 2 * uly)

    prior = lax.rem(b + cells - 1, cells)
    following = lax.rem(b + 1, cells)
    my_group = group_of(b, u)
    prior_uly = group_of(prior, my_group)
    following_uly = group_of(following, my_group)
    sideways = (
        {"blk": prior, "uly": prior_uly},
        {"blk": following, "uly": following_uly},
    )

    def peer(step):
        return lax.rem(u + step, ulys)

    listens = lax.rem(b + 1, 2)
    barrier = pltpu.get_barrier_semaphore()
    for step in range(1, ulys):
        to = peer(step)

        @pl.when((to < u) | ((u == ulys - 2) & (to == ulys - 1)))
        def _():
            pl.semaphore_signal(barrier, inc=1, device_id={"uly": to}, device_id_type=MESH)

    @pl.when(listens == 0)
    def _():
        for side in sideways:
            pl.semaphore_signal(barrier, inc=1, device_id=side, device_id_type=MESH)

    mask_rows = (b * per_cell // 8) * 8
    mask_copy = pltpu.make_async_copy(
        mask_hbm.at[pl.ds(pl.multiple_of(mask_rows, 8), 8), :], mask, mask_sem
    )
    mask_copy.start()

    sources = (k_hbm, v_hbm, q_hbm, g_hbm)

    def landing(head, which, uly):
        at = pl.ds(pl.multiple_of(uly * rows, rows), rows)
        if which < 2:
            return kv.at[head, which, 1, at, :]
        return qg.at[head, which - 2, at, :]

    def columns_of(group, head):
        start = (group * HEADS_HERE + head) * DIM
        return pl.ds(pl.multiple_of(start, DIM), DIM)

    def entry_local(head, which):
        return pltpu.make_async_copy(
            sources[which].at[:, columns_of(my_group, head)],
            landing(head, which, u),
            local_sem.at[head, which],
        )

    def entry_copy(head, which, step):
        to = peer(step)
        return pltpu.make_async_remote_copy(
            src_ref=sources[which].at[:, columns_of(group_of(b, to), head)],
            dst_ref=landing(head, which, u),
            send_sem=in_send.at[head, which, step - 1],
            recv_sem=in_recv.at[head, which, step - 1],
            device_id={"uly": to},
            device_id_type=MESH,
        )

    def entry_arrival(head, which, step):
        came_from = lax.rem(u + ulys - step, ulys)
        return pltpu.make_async_remote_copy(
            src_ref=sources[which].at[:, columns_of(my_group, head)],
            dst_ref=landing(head, which, came_from),
            send_sem=in_send.at[head, which, step - 1],
            recv_sem=in_recv.at[head, which, step - 1],
            device_id={"uly": came_from},
            device_id_type=MESH,
        )

    for which in range(4):
        for head in range(HEADS_HERE):
            entry_local(head, which).start()

    pl.semaphore_wait(barrier, jnp.where(u == ulys - 1, 1, ulys - 1 - u) + 2 * listens)
    for step in range(1, ulys):
        to = peer(step)

        @pl.when(to > u)
        def _():
            pl.semaphore_signal(
                ready.at[step - 1], inc=1, device_id={"uly": to}, device_id_type=MESH
            )

    @pl.when(listens == 1)
    def _():
        for side in range(2):
            pl.semaphore_signal(
                ready_side.at[1 - side], inc=1, device_id=sideways[side], device_id_type=MESH
            )

    for last in (False, True):
        for step in range(1, ulys):
            to = peer(step)

            @pl.when((to < u) & ((to == 0) == last))
            def _():
                pl.semaphore_wait(ready.at[ulys - 1 - step], 1)

        for head in range(HEADS_HERE):
            for which in range(2):
                for step in range(1, ulys):

                    @pl.when((peer(step) == 0) == last)
                    def _():
                        entry_copy(head, which, step).start()

    def start_rest(head):
        for which in range(2, 4):
            for step in range(1, ulys):
                entry_copy(head, which, step).start()

    def await_entry(head, which):
        entry_local(head, which).wait()
        for step in range(1, ulys):
            entry_arrival(head, which, step).wait_recv()

    def band_copy(head, which, side):
        return pltpu.make_async_remote_copy(
            src_ref=kv.at[head, which, 1],
            dst_ref=kv.at[head, which, 2 - 2 * side],
            send_sem=band_send.at[head, which, side],
            recv_sem=band_recv.at[head, which, side],
            device_id=sideways[side],
            device_id_type=MESH,
        )

    def band_arrival(head, which, side):
        return pltpu.make_async_remote_copy(
            src_ref=kv.at[head, which, 1],
            dst_ref=kv.at[head, which, 2 - 2 * side],
            send_sem=band_send.at[head, which, side],
            recv_sem=band_recv.at[head, which, side],
            device_id=sideways[side],
            device_id_type=MESH,
        )

    def send_band(head):
        for which in range(2):
            for side in range(2):
                band_copy(head, which, side).start()

    def part_copy(head, which, side):
        return pltpu.make_async_remote_copy(
            src_ref=sides.at[head, which, side],
            dst_ref=landed.at[head, which, 1 - side],
            send_sem=part_send.at[head, which, side],
            recv_sem=part_recv.at[head, which, side],
            device_id=sideways[side],
            device_id_type=MESH,
        )

    outs = (dq_hbm, dk_hbm, dv_hbm)

    def exit_local(head, which):
        return pltpu.make_async_copy(
            results.at[head, which, pl.ds(pl.multiple_of(u * rows, rows), rows), :],
            outs[which].at[:, columns_of(my_group, head)],
            out_local.at[head, which],
        )

    def exit_copy(head, which, step):
        to = peer(step)
        return pltpu.make_async_remote_copy(
            src_ref=results.at[head, which, pl.ds(pl.multiple_of(to * rows, rows), rows), :],
            dst_ref=outs[which].at[:, columns_of(my_group, head)],
            send_sem=out_send.at[head, which, step - 1],
            recv_sem=out_recv.at[head, which, step - 1],
            device_id={"uly": to},
            device_id_type=MESH,
        )

    def exit_arrival(head, which, step):
        came_from = lax.rem(u + ulys - step, ulys)
        return pltpu.make_async_remote_copy(
            src_ref=results.at[head, which, pl.ds(0, rows), :],
            dst_ref=outs[which].at[:, columns_of(group_of(b, came_from), head)],
            send_sem=out_send.at[head, which, step - 1],
            recv_sem=out_recv.at[head, which, step - 1],
            device_id={"uly": came_from},
            device_id_type=MESH,
        )

    def send_out(head, which):
        exit_local(head, which).start()
        for step in range(1, ulys):
            exit_copy(head, which, step).start()

    scale = 1.0 / math.sqrt(DIM)
    scale2 = scale * math.log2(math.e)
    first_row = lax.rem(b * per_cell, 8)
    near = (prior, b, following)

    def bias_row(part, block):
        pieces = []
        for a in range(per_cell):
            allowed = mask[first_row + a, near[part] * per_cell + block] > 0
            pieces.append(jnp.full((1, BLOCK), jnp.where(allowed, 0.0, -1e30), F32))
        return jnp.concatenate(pieces, axis=1)

    parts = [(part, block) for part in range(3) for block in range(per_cell)]

    def block_rows(block):
        return slice(block * BLOCK, (block + 1) * BLOCK)

    def softmax(head):
        q = qg[head, 0]
        top = None
        for part, block in parts:
            at = block_rows(block)
            s = times_t(kv[head, 0, part, at, :], q) * scale2 + bias_row(part, block)
            scores[head, part, at, :] = s
            here = groups_max(s)
            top = here if top is None else jnp.maximum(top, here)
        top = jnp.max(top, axis=0, keepdims=True)
        total = jnp.zeros((8, genes), F32)
        for part, block in parts:
            at = block_rows(block)
            e = jnp.exp2(scores[head, part, at, :] - top)
            scores[head, part, at, :] = e
            total += groups_sum(e)
        inverse = 1.0 / jnp.sum(total, axis=0, keepdims=True)
        for part, block in parts:
            at = block_rows(block)
            probs_low[head, part, at, :] = (scores[head, part, at, :] * inverse).astype(BF16)
        return inverse

    def gradients(head, inverse):
        q = qg[head, 0]
        g = qg[head, 1]
        for side in range(2):
            sides[head, 1, side] = jnp.dot(
                probs_low[head, 2 * side], g, preferred_element_type=F32
            ).astype(BF16)
            part_copy(head, 1, side).start()
        delta = jnp.zeros((8, genes), F32)
        for part, block in parts:
            at = block_rows(block)
            d = times_t(kv[head, 1, part, at, :], g)
            dprobs[part, at, :] = d
            delta += groups_sum(scores[head, part, at, :] * d)
        delta = jnp.sum(delta, axis=0, keepdims=True) * inverse
        for part, block in parts:
            at = block_rows(block)
            p = scores[head, part, at, :] * inverse
            dscores[part, at, :] = (p * (dprobs[part, at, :] - delta)).astype(BF16)
        for side in range(2):
            sides[head, 0, side] = jnp.dot(
                dscores[2 * side], q, preferred_element_type=F32
            ).astype(BF16)
            part_copy(head, 0, side).start()
        grad = jnp.zeros((DIM, genes), F32)
        for part in range(3):
            grad += jnp.dot(kv[head, 0, part].T, dscores[part], preferred_element_type=F32)
        results[head, 0] = (grad.T * scale).astype(BF16)
        own[head, 1] = jnp.dot(probs_low[head, 1], g, preferred_element_type=F32)
        own[head, 0] = jnp.dot(dscores[1], q, preferred_element_type=F32)

    def finish(head):
        for which, factor in ((1, None), (0, scale)):
            for side in range(2):
                part_copy(head, which, side).wait_recv()
            summed = (
                own[head, which]
                + landed[head, which, 1].astype(F32)
                + landed[head, which, 0].astype(F32)
            )
            if factor is not None:
                summed = summed * factor
            results[head, 1 + which] = summed.astype(BF16)
            send_out(head, 1 + which)

    def await_band(head, which):
        for side in range(2):
            band_arrival(head, which, side).wait_recv()

    mask_copy.wait()

    for which in range(2):
        await_entry(0, which)
    start_rest(0)

    @pl.when(listens == 0)
    def _():
        for side in range(2):
            pl.semaphore_wait(ready_side.at[side], 1)

    send_band(0)
    for which in range(2):
        await_entry(1, which)
    start_rest(1)
    send_band(1)
    await_entry(0, 2)
    await_band(0, 0)
    inverse = softmax(0)
    await_entry(0, 3)
    await_band(0, 1)
    gradients(0, inverse)
    await_entry(1, 2)
    await_band(1, 0)
    inverse = softmax(1)
    await_entry(1, 3)
    send_out(0, 0)
    await_band(1, 1)
    gradients(1, inverse)
    finish(0)
    send_out(1, 0)
    finish(1)

    for head in range(HEADS_HERE):
        for which in range(4):
            for step in range(1, ulys):
                entry_copy(head, which, step).wait_send()
        for which in range(2):
            for side in range(2):
                band_copy(head, which, side).wait_send()
                part_copy(head, which, side).wait_send()
        for which in range(3):
            exit_local(head, which).wait()
            for step in range(1, ulys):
                exit_copy(head, which, step).wait_send()
                exit_arrival(head, which, step).wait_recv()


def settle(dq, dk, dv, dq_out, dk_out, dv_out, sems):
    pairs = ((dq, dq_out), (dk, dk_out), (dv, dv_out))
    copies = [pltpu.make_async_copy(*pair, sems.at[i]) for i, pair in enumerate(pairs)]
    for copy in copies:
        copy.start()
    for copy in copies:
        copy.wait()


def local(cells, ulys, queries, keys, values, out_grad, block_mask):
    rows, width = queries.shape
    genes = rows * ulys
    n = HEADS_HERE
    dma = pltpu.SemaphoreType.DMA
    outputs = [jax.ShapeDtypeStruct((rows, width), BF16)] * 3
    grads = pl.pallas_call(
        functools.partial(kernel, cells, ulys),
        out_shape=outputs,
        in_specs=[pl.BlockSpec(memory_space=pltpu.HBM)] * 5,
        out_specs=[pl.BlockSpec(memory_space=pl.ANY)] * 3,
        scratch_shapes=[
            pltpu.VMEM((n, 2, 3, genes, DIM), BF16),
            pltpu.VMEM((n, 2, genes, DIM), BF16),
            pltpu.VMEM((n, 3, genes, genes), F32),
            pltpu.VMEM((3, genes, genes), F32),
            pltpu.VMEM((n, 3, genes, genes), BF16),
            pltpu.VMEM((3, genes, genes), BF16),
            pltpu.VMEM((n, 2, genes, DIM), F32),
            pltpu.VMEM((n, 2, 2, genes, DIM), BF16),
            pltpu.VMEM((n, 2, 2, genes, DIM), BF16),
            pltpu.VMEM((n, 3, genes, DIM), BF16),
            pltpu.SMEM((8, block_mask.shape[1]), jnp.int32),
            dma,
            pltpu.SemaphoreType.REGULAR((ulys - 1,)),
            pltpu.SemaphoreType.REGULAR((2,)),
            dma((n, 4)),
            dma((n, 4, ulys - 1)),
            dma((n, 4, ulys - 1)),
            dma((n, 2, 2)),
            dma((n, 2, 2)),
            dma((n, 2, 2)),
            dma((n, 2, 2)),
            dma((n, 3)),
            dma((n, 3, ulys - 1)),
            dma((n, 3, ulys - 1)),
        ],
        compiler_params=pltpu.CompilerParams(
            collective_id=0, has_side_effects=True, vmem_limit_bytes=40 * 1024 * 1024
        ),
    )(*(pltpu.with_memory_space_constraint(x, pltpu.HBM) for x in (queries, keys, values, out_grad, block_mask)))
    return pl.pallas_call(
        settle,
        out_shape=outputs,
        in_specs=[pl.BlockSpec(memory_space=pl.ANY)] * 3,
        out_specs=[pl.BlockSpec(memory_space=pltpu.HBM)] * 3,
        scratch_shapes=[dma((3,))],
        compiler_params=pltpu.CompilerParams(vmem_limit_bytes=1024 * 1024),
    )(*grads)


def solution(mesh):
    rows = P(("batch", "blk", "uly"), None)
    return jax.shard_map(
        functools.partial(local, mesh.shape["blk"], mesh.shape["uly"]),
        mesh=mesh,
        in_specs=(rows, rows, rows, rows, P("batch", None)),
        out_specs=(rows, rows, rows),
        check_vma=False,
    )
```

```python
import functools
import math

import jax
import jax.numpy as jnp
from jax import lax
from jax.experimental import pallas as pl
from jax.experimental.pallas import tpu as pltpu
from jax.sharding import PartitionSpec as P

MESH = pl.DeviceIdType.MESH
DIM = 128
BLOCK = 128
HEADS_HERE = 2
F32 = jnp.float32
BF16 = jnp.bfloat16


def times_t(left, right):
    return lax.dot_general(left, right, (((1,), (1,)), ((), ())), preferred_element_type=F32)


def groups_sum(block):
    rows, columns = block.shape
    return jnp.sum(block.reshape(rows // 8, 8, columns), axis=0)


def groups_max(block):
    rows, columns = block.shape
    return jnp.max(block.reshape(rows // 8, 8, columns), axis=0)


def kernel(
    cells,
    ulys,
    q_hbm,
    k_hbm,
    v_hbm,
    g_hbm,
    mask_hbm,
    dq_hbm,
    dk_hbm,
    dv_hbm,
    kv,
    qg,
    scores,
    dprobs,
    probs_low,
    dscores,
    own,
    sides,
    landed,
    results,
    mask,
    mask_sem,
    ready,
    ready_side,
    local_sem,
    in_send,
    in_recv,
    band_send,
    band_recv,
    part_send,
    part_recv,
    out_local,
    out_send,
    out_recv,
):
    b = lax.axis_index("blk")
    u = lax.axis_index("uly")
    rows = q_hbm.shape[0]
    genes = rows * ulys
    per_cell = genes // BLOCK
    half = cells // 2

    def group_of(blk, uly):
        upper = blk // half
        return uly + upper * (ulys - 1 - 2 * uly)

    prior = lax.rem(b + cells - 1, cells)
    following = lax.rem(b + 1, cells)
    my_group = group_of(b, u)
    prior_uly = group_of(prior, my_group)
    following_uly = group_of(following, my_group)
    sideways = (
        {"blk": prior, "uly": prior_uly},
        {"blk": following, "uly": following_uly},
    )

    def peer(step):
        return lax.rem(u + step, ulys)

    listens = lax.rem(b + 1, 2)
    barrier = pltpu.get_barrier_semaphore()
    for step in range(1, ulys):
        to = peer(step)

        @pl.when((to < u) | ((u == ulys - 2) & (to == ulys - 1)))
        def _():
            pl.semaphore_signal(barrier, inc=1, device_id={"uly": to}, device_id_type=MESH)

    @pl.when(listens == 0)
    def _():
        for side in sideways:
            pl.semaphore_signal(barrier, inc=1, device_id=side, device_id_type=MESH)

    mask_rows = (b * per_cell // 8) * 8
    mask_copy = pltpu.make_async_copy(
        mask_hbm.at[pl.ds(pl.multiple_of(mask_rows, 8), 8), :], mask, mask_sem
    )
    mask_copy.start()

    sources = (k_hbm, v_hbm, q_hbm, g_hbm)

    def landing(head, which, uly):
        at = pl.ds(pl.multiple_of(uly * rows, rows), rows)
        if which < 2:
            return kv.at[head, which, 1, at, :]
        return qg.at[head, which - 2, at, :]

    def columns_of(group, head):
        start = (group * HEADS_HERE + head) * DIM
        return pl.ds(pl.multiple_of(start, DIM), DIM)

    def entry_local(head, which):
        return pltpu.make_async_copy(
            sources[which].at[:, columns_of(my_group, head)],
            landing(head, which, u),
            local_sem.at[head, which],
        )

    def entry_copy(head, which, step):
        to = peer(step)
        return pltpu.make_async_remote_copy(
            src_ref=sources[which].at[:, columns_of(group_of(b, to), head)],
            dst_ref=landing(head, which, u),
            send_sem=in_send.at[head, which, step - 1],
            recv_sem=in_recv.at[head, which, step - 1],
            device_id={"uly": to},
            device_id_type=MESH,
        )

    def entry_arrival(head, which, step):
        came_from = lax.rem(u + ulys - step, ulys)
        return pltpu.make_async_remote_copy(
            src_ref=sources[which].at[:, columns_of(my_group, head)],
            dst_ref=landing(head, which, came_from),
            send_sem=in_send.at[head, which, step - 1],
            recv_sem=in_recv.at[head, which, step - 1],
            device_id={"uly": came_from},
            device_id_type=MESH,
        )

    for which in range(4):
        for head in range(HEADS_HERE):
            entry_local(head, which).start()

    pl.semaphore_wait(barrier, jnp.where(u == ulys - 1, 1, ulys - 1 - u) + 2 * listens)
    for step in range(1, ulys):
        to = peer(step)

        @pl.when(to > u)
        def _():
            pl.semaphore_signal(
                ready.at[step - 1], inc=1, device_id={"uly": to}, device_id_type=MESH
            )

    @pl.when(listens == 1)
    def _():
        for side in range(2):
            pl.semaphore_signal(
                ready_side.at[1 - side], inc=1, device_id=sideways[side], device_id_type=MESH
            )

    for last in (False, True):
        for step in range(1, ulys):
            to = peer(step)

            @pl.when((to < u) & ((to == 0) == last))
            def _():
                pl.semaphore_wait(ready.at[ulys - 1 - step], 1)

        for head in range(HEADS_HERE):
            for which in range(2):
                for step in range(1, ulys):

                    @pl.when((peer(step) == 0) == last)
                    def _():
                        entry_copy(head, which, step).start()

    def start_rest(head, which):
        for step in range(1, ulys):
            entry_copy(head, which, step).start()

    def await_entry(head, which):
        entry_local(head, which).wait()
        for step in range(1, ulys):
            entry_arrival(head, which, step).wait_recv()

    def band_copy(head, which, side):
        return pltpu.make_async_remote_copy(
            src_ref=kv.at[head, which, 1],
            dst_ref=kv.at[head, which, 2 - 2 * side],
            send_sem=band_send.at[head, which, side],
            recv_sem=band_recv.at[head, which, side],
            device_id=sideways[side],
            device_id_type=MESH,
        )

    def band_arrival(head, which, side):
        return pltpu.make_async_remote_copy(
            src_ref=kv.at[head, which, 1],
            dst_ref=kv.at[head, which, 2 - 2 * side],
            send_sem=band_send.at[head, which, side],
            recv_sem=band_recv.at[head, which, side],
            device_id=sideways[side],
            device_id_type=MESH,
        )

    def send_band(head):
        for which in range(2):
            for side in range(2):
                band_copy(head, which, side).start()

    def part_copy(head, which, side):
        return pltpu.make_async_remote_copy(
            src_ref=sides.at[head, which, side],
            dst_ref=landed.at[head, which, 1 - side],
            send_sem=part_send.at[head, which, side],
            recv_sem=part_recv.at[head, which, side],
            device_id=sideways[side],
            device_id_type=MESH,
        )

    outs = (dq_hbm, dk_hbm, dv_hbm)

    def exit_local(head, which):
        return pltpu.make_async_copy(
            results.at[head, which, pl.ds(pl.multiple_of(u * rows, rows), rows), :],
            outs[which].at[:, columns_of(my_group, head)],
            out_local.at[head, which],
        )

    def exit_copy(head, which, step):
        to = peer(step)
        return pltpu.make_async_remote_copy(
            src_ref=results.at[head, which, pl.ds(pl.multiple_of(to * rows, rows), rows), :],
            dst_ref=outs[which].at[:, columns_of(my_group, head)],
            send_sem=out_send.at[head, which, step - 1],
            recv_sem=out_recv.at[head, which, step - 1],
            device_id={"uly": to},
            device_id_type=MESH,
        )

    def exit_arrival(head, which, step):
        came_from = lax.rem(u + ulys - step, ulys)
        return pltpu.make_async_remote_copy(
            src_ref=results.at[head, which, pl.ds(0, rows), :],
            dst_ref=outs[which].at[:, columns_of(group_of(b, came_from), head)],
            send_sem=out_send.at[head, which, step - 1],
            recv_sem=out_recv.at[head, which, step - 1],
            device_id={"uly": came_from},
            device_id_type=MESH,
        )

    def send_out(head, which):
        exit_local(head, which).start()
        for step in range(1, ulys):
            exit_copy(head, which, step).start()

    scale = 1.0 / math.sqrt(DIM)
    scale2 = scale * math.log2(math.e)
    first_row = lax.rem(b * per_cell, 8)
    near = (prior, b, following)

    def bias_row(part, block):
        pieces = []
        for a in range(per_cell):
            allowed = mask[first_row + a, near[part] * per_cell + block] > 0
            pieces.append(jnp.full((1, BLOCK), jnp.where(allowed, 0.0, -1e30), F32))
        return jnp.concatenate(pieces, axis=1)

    parts = [(part, block) for part in range(3) for block in range(per_cell)]

    def block_rows(block):
        return slice(block * BLOCK, (block + 1) * BLOCK)

    def softmax(head):
        q = qg[head, 0]
        top = None
        for part, block in parts:
            at = block_rows(block)
            s = times_t(kv[head, 0, part, at, :], q) * scale2 + bias_row(part, block)
            scores[head, part, at, :] = s
            here = groups_max(s)
            top = here if top is None else jnp.maximum(top, here)
        top = jnp.max(top, axis=0, keepdims=True)
        total = jnp.zeros((8, genes), F32)
        for part, block in parts:
            at = block_rows(block)
            e = jnp.exp2(scores[head, part, at, :] - top)
            scores[head, part, at, :] = e
            total += groups_sum(e)
        inverse = 1.0 / jnp.sum(total, axis=0, keepdims=True)
        for part, block in parts:
            at = block_rows(block)
            probs_low[head, part, at, :] = (scores[head, part, at, :] * inverse).astype(BF16)
        return inverse

    def gradients(head, inverse):
        q = qg[head, 0]
        g = qg[head, 1]
        for side in range(2):
            sides[head, 1, side] = jnp.dot(
                probs_low[head, 2 * side], g, preferred_element_type=F32
            ).astype(BF16)
            part_copy(head, 1, side).start()
        delta = jnp.zeros((8, genes), F32)
        for part, block in parts:
            at = block_rows(block)
            d = times_t(kv[head, 1, part, at, :], g)
            dprobs[part, at, :] = d
            delta += groups_sum(scores[head, part, at, :] * d)
        delta = jnp.sum(delta, axis=0, keepdims=True) * inverse
        for part, block in parts:
            at = block_rows(block)
            p = scores[head, part, at, :] * inverse
            dscores[part, at, :] = (p * (dprobs[part, at, :] - delta)).astype(BF16)
        for side in range(2):
            sides[head, 0, side] = jnp.dot(
                dscores[2 * side], q, preferred_element_type=F32
            ).astype(BF16)
            part_copy(head, 0, side).start()
        grad = jnp.zeros((DIM, genes), F32)
        for part in range(3):
            grad += jnp.dot(kv[head, 0, part].T, dscores[part], preferred_element_type=F32)
        results[head, 0] = (grad.T * scale).astype(BF16)
        own[head, 1] = jnp.dot(probs_low[head, 1], g, preferred_element_type=F32)
        own[head, 0] = jnp.dot(dscores[1], q, preferred_element_type=F32)

    def finish(head):
        for which, factor in ((1, None), (0, scale)):
            for side in range(2):
                part_copy(head, which, side).wait_recv()
            summed = (
                own[head, which]
                + landed[head, which, 1].astype(F32)
                + landed[head, which, 0].astype(F32)
            )
            if factor is not None:
                summed = summed * factor
            results[head, 1 + which] = summed.astype(BF16)
            send_out(head, 1 + which)

    def await_band(head, which):
        for side in range(2):
            band_arrival(head, which, side).wait_recv()

    mask_copy.wait()

    for which in range(2):
        await_entry(0, which)
        start_rest(0, which + 2)

    @pl.when(listens == 0)
    def _():
        for side in range(2):
            pl.semaphore_wait(ready_side.at[side], 1)

    send_band(0)
    for which in range(2):
        await_entry(1, which)
        start_rest(1, which + 2)
    send_band(1)
    await_entry(0, 2)
    await_band(0, 0)
    inverse = softmax(0)
    await_entry(0, 3)
    await_band(0, 1)
    gradients(0, inverse)
    await_entry(1, 2)
    await_band(1, 0)
    inverse = softmax(1)
    await_entry(1, 3)
    send_out(0, 0)
    await_band(1, 1)
    gradients(1, inverse)
    finish(0)
    send_out(1, 0)
    finish(1)

    for head in range(HEADS_HERE):
        for which in range(4):
            for step in range(1, ulys):
                entry_copy(head, which, step).wait_send()
        for which in range(2):
            for side in range(2):
                band_copy(head, which, side).wait_send()
                part_copy(head, which, side).wait_send()
        for which in range(3):
            exit_local(head, which).wait()
            for step in range(1, ulys):
                exit_copy(head, which, step).wait_send()
                exit_arrival(head, which, step).wait_recv()


def settle(dq, dk, dv, dq_out, dk_out, dv_out, sems):
    pairs = ((dq, dq_out), (dk, dk_out), (dv, dv_out))
    copies = [pltpu.make_async_copy(*pair, sems.at[i]) for i, pair in enumerate(pairs)]
    for copy in copies:
        copy.start()
    for copy in copies:
        copy.wait()


def local(cells, ulys, queries, keys, values, out_grad, block_mask):
    rows, width = queries.shape
    genes = rows * ulys
    n = HEADS_HERE
    dma = pltpu.SemaphoreType.DMA
    outputs = [jax.ShapeDtypeStruct((rows, width), BF16)] * 3
    grads = pl.pallas_call(
        functools.partial(kernel, cells, ulys),
        out_shape=outputs,
        in_specs=[pl.BlockSpec(memory_space=pltpu.HBM)] * 5,
        out_specs=[pl.BlockSpec(memory_space=pl.ANY)] * 3,
        scratch_shapes=[
            pltpu.VMEM((n, 2, 3, genes, DIM), BF16),
            pltpu.VMEM((n, 2, genes, DIM), BF16),
            pltpu.VMEM((n, 3, genes, genes), F32),
            pltpu.VMEM((3, genes, genes), F32),
            pltpu.VMEM((n, 3, genes, genes), BF16),
            pltpu.VMEM((3, genes, genes), BF16),
            pltpu.VMEM((n, 2, genes, DIM), F32),
            pltpu.VMEM((n, 2, 2, genes, DIM), BF16),
            pltpu.VMEM((n, 2, 2, genes, DIM), BF16),
            pltpu.VMEM((n, 3, genes, DIM), BF16),
            pltpu.SMEM((8, block_mask.shape[1]), jnp.int32),
            dma,
            pltpu.SemaphoreType.REGULAR((ulys - 1,)),
            pltpu.SemaphoreType.REGULAR((2,)),
            dma((n, 4)),
            dma((n, 4, ulys - 1)),
            dma((n, 4, ulys - 1)),
            dma((n, 2, 2)),
            dma((n, 2, 2)),
            dma((n, 2, 2)),
            dma((n, 2, 2)),
            dma((n, 3)),
            dma((n, 3, ulys - 1)),
            dma((n, 3, ulys - 1)),
        ],
        compiler_params=pltpu.CompilerParams(
            collective_id=0, has_side_effects=True, vmem_limit_bytes=40 * 1024 * 1024
        ),
    )(*(pltpu.with_memory_space_constraint(x, pltpu.HBM) for x in (queries, keys, values, out_grad, block_mask)))
    return pl.pallas_call(
        settle,
        out_shape=outputs,
        in_specs=[pl.BlockSpec(memory_space=pl.ANY)] * 3,
        out_specs=[pl.BlockSpec(memory_space=pltpu.HBM)] * 3,
        scratch_shapes=[dma((3,))],
        compiler_params=pltpu.CompilerParams(vmem_limit_bytes=1024 * 1024),
    )(*grads)


def solution(mesh):
    rows = P(("batch", "blk", "uly"), None)
    return jax.shard_map(
        functools.partial(local, mesh.shape["blk"], mesh.shape["uly"]),
        mesh=mesh,
        in_specs=(rows, rows, rows, rows, P("batch", None)),
        out_specs=(rows, rows, rows),
        check_vma=False,
    )
```
